512 devices in a mesh: ep: 64 (over y, x, core), tp: 8 (over z).
Axes of the slice: x: 4, y: 8, z: 8, core: 2. Of those that a mesh axis runs over, the one named last changes fastest.
Arguments:
- attn: bfloat16 [512, 4096], P('ep', 'tp'), may hold values from -6 to 6
- resid: bfloat16 [512, 4096], P('ep'), may hold values from -3 to 3
- wo: bfloat16 [4096, 4096], P('tp', 'ep'), may hold values from -0.09375 to 0.09375
- norm_gain: float32 [4096], replicated, may hold values from 0.25 to 1.75
- router: bfloat16 [4096, 8], replicated, may hold values from -0.09375 to 0.09375
- expert_ids: int32 [512, 2], P('ep'), may hold values from 0 to 7, all different within a row; in each aligned block of 8 rows (0 to 7, 8 to 15, ...) at most 4 rows name the same one
- w_gate: bfloat16 [4096, 65536], P(None, ('ep', 'tp')), may hold values from -0.09375 to 0.09375
- w_up: bfloat16 [4096, 65536], P(None, ('ep', 'tp')), may hold values from -0.09375 to 0.09375
- w_down: bfloat16 [65536, 4096], P(('ep', 'tp')), may hold values from -0.1875 to 0.1875
- lengths: int32 [64, 4], P('ep'), may hold values from 1 to 4, 8 in all within a row
- final_gain: float32 [4096], replicated, may hold values from 0.25 to 1.75
- head: bfloat16 [16384, 4096], P(('ep', 'tp')), may hold values from -0.375 to 0.375
Outputs:
- mixed: bfloat16 [512, 4096], P('ep')
- max_logit: float32 [256], replicated
The draws below stay inside these ranges and needn't reach their ends.
Inputs may be any that keep to these rules, and one draw needn't show every extreme that they name: `expert_ids`: the two ids of a row differ; among the 8 rows of one index of ep no expert is named by more than 4 rows, a bound that some block reaches. Each row of lengths sums to 8, and its largest entry is 4.
All inputs are finite; a program needn't handle non-finite values.
Results may differ from the reference program's by a relative error of at most 0.0075.
Values may be sent and summed in bfloat16 or wider, within the bound.
A program may use at most 192 MiB of HBM per device.

```python
import math
import jax
import jax.numpy as jnp
import numpy as np
from jax import lax

D = 4096
EXPERTS = 8
TOPK = 2
FF = 8192
VOCAB = 16384
ROWS = 8
REQ_DEV = 4
CAP = 4
TOKENS = 512
FF_DEV = 128
N_EP = 64


def level_of(stream_key, shape, cuts, low, largest):
    def one(position, parts):
        heights = jax.random.uniform(jax.random.fold_in(jax.random.fold_in(stream_key, 6), position), (parts,), jnp.float32, low / len(cuts), largest / len(cuts))
        return jnp.repeat(jnp.exp(heights), shape[position] // parts).reshape((-1,) + (1,) * (len(shape) - position - 1))

    loudness = one(*cuts[0])
    for cut in cuts[1:]:
        loudness = loudness * one(*cut)
    return loudness


def profile(amount, total, limit, slope):
    weights = [(1 << 20) // math.isqrt(standing ** slope) + 1 for standing in range(2, amount + 1)]
    rest, given = total - limit - (amount - 1), [1] * (amount - 1)
    while rest > 0:
        candidates = [i for i in range(amount - 1) if given[i] < limit]
        mass, remaining = sum([weights[i] for i in candidates]), rest
        for i in candidates:
            extra = min(limit - given[i], max(1, remaining * weights[i] // mass), rest)
            given[i] = given[i] + extra
            rest = rest - extra
    return np.array([limit] + given)


def uneven(rng, number_of, total, limit, lean):
    if number_of == 2:
        one = jax.random.randint(rng, (), max(1, total - limit), min(limit, total - 1) + 1)
        return jnp.stack([one, total - one])
    sizes = jnp.asarray(profile(number_of, total, limit, lean), jnp.int32)
    couples = (number_of - 1) // 2
    giver, taker = sizes[1:1 + 2 * couples:2], sizes[2:2 + 2 * couples:2]
    room = jnp.minimum(giver - 1, limit - taker)
    shifted = jax.random.randint(jax.random.fold_in(rng, 1), (couples,), 0, 1 << 20) % (room + 1)
    sizes = sizes.at[1:1 + 2 * couples:2].set(giver - shifted).at[2:2 + 2 * couples:2].set(taker + shifted)
    return sizes[jax.random.permutation(jax.random.fold_in(rng, 2), number_of)]


def shared_out(own_key, own, number, rows, amount, top, limit, skew):
    ranking = jax.random.permutation(own_key, amount)
    crowded, common = portions_of(amount, rows * top, limit, skew, True), portions_of(amount, rows * top, limit, skew, False)
    places = jnp.arange(amount)

    def named(sizes, offset_by):
        used = int((sizes > 0).sum())
        fixed = max(1, used // 4)
        shifted = fixed + (places - fixed + offset_by * (used - fixed)) % max(1, amount - fixed)
        return jnp.zeros((amount,), jnp.int32).at[ranking[jnp.where(places < fixed, places, shifted)]].set(jnp.asarray(sizes, jnp.int32))

    sizes = jnp.where(number % 4 == 0, named(crowded, number // 4), named(common, number - number // 4 - 1))
    mixed = jax.random.permutation(jax.random.fold_in(own, 3), amount)
    donor, taker = mixed[0:amount // 2 * 2:2], mixed[1:amount // 2 * 2:2]
    slack = jnp.minimum(sizes[donor] - 1, limit - sizes[taker]) // 2
    slack = jnp.where((donor == ranking[0]) | (taker == ranking[0]) | (sizes[taker] == 0), 0, jnp.maximum(slack, 0))
    shifted = jax.random.randint(jax.random.fold_in(own, 4), (amount // 2,), 0, 1 << 20) % (slack + 1)
    sizes = sizes.at[donor].add(-shifted).at[taker].add(shifted)
    labels = jnp.searchsorted(jnp.cumsum(sizes), jnp.arange(rows * top), side="right").astype(jnp.int32)
    listing = labels.reshape(top, rows).T
    listing = listing[jax.random.permutation(jax.random.fold_in(own, 1), rows)]
    offset_by = jax.random.randint(jax.random.fold_in(own, 2), (rows, 1), 0, top)
    return jnp.take_along_axis(listing, (jnp.arange(top)[None, :] + offset_by) % top, axis=1)


def portions_of(count, total, bound, lean, full):
    loads = [(1 << 20) // math.isqrt(standing ** lean) + 1 for standing in range(1, count + 1)]
    largest = bound if full else min(bound, max(-(-total // count), total * loads[0] // sum(loads)))
    least = 1 if total - largest >= count - 1 else 0
    counts, spare = [largest] + [least] * (count - 1), total - largest - least * (count - 1)
    while spare > 0:
        candidates = [i for i in range(1, count) if counts[i] < largest] or [i for i in range(1, count) if counts[i] < bound]
        pool, budget = sum([loads[i] for i in candidates]), spare
        for i in candidates:
            extra = min(bound - counts[i], max(1, budget * loads[i] // pool), spare)
            counts[i] = counts[i] + extra
            spare = spare - extra
    return np.array(counts)


def bell_draw(key, extent, spread, most, pieces=(), kind=jnp.bfloat16):
    drawn = spread * jax.random.normal(key, extent, jnp.float32)
    if pieces:
        drawn = drawn * level_of(key, extent, pieces, -0.22, 0.18)
    return jnp.clip(drawn, -most, most).astype(kind)


def setup_inputs(seed: int = 0) -> dict:
    arg_keys = jax.random.split(jax.random.key(seed), 13)
    attn = bell_draw(arg_keys[0], (TOKENS, D), 1.0, 6.0, ((0, 64), (1, 8)))
    resid = bell_draw(arg_keys[1], (TOKENS, D), 0.5, 3.0, ((0, 64),))
    wo = bell_draw(arg_keys[2], (D, D), D ** -0.5, 0.09375, ((0, 8), (1, 64)))
    norm_gain = jnp.clip(1.0 + 0.15 * jax.random.normal(arg_keys[3], (D,), jnp.float32), 0.25, 1.75)
    router = bell_draw(arg_keys[4], (D, EXPERTS), D ** -0.5, 0.09375)
    expert_ids_keys = jax.random.split(jax.random.fold_in(arg_keys[5], 1), TOKENS // ROWS)
    expert_ids_turns = jax.random.permutation(jax.random.fold_in(arg_keys[5], 3), TOKENS // ROWS)
    expert_ids = jax.vmap(lambda own, number: shared_out(jax.random.fold_in(arg_keys[5], 2), own, number, ROWS, EXPERTS, TOPK, CAP, 2))(expert_ids_keys, expert_ids_turns).reshape((TOKENS, TOPK))
    w_gate = bell_draw(arg_keys[6], (D, EXPERTS * FF), D ** -0.5, 0.09375, ((1, 512),))
    w_up = bell_draw(arg_keys[7], (D, EXPERTS * FF), D ** -0.5, 0.09375, ((1, 512),))
    w_down = bell_draw(arg_keys[8], (EXPERTS * FF, D), (FF // 8) ** -0.5, 0.1875, ((0, 512),))
    lengths = jax.vmap(lambda own: uneven(own, REQ_DEV, ROWS, ROWS // 2, 2))(jax.random.split(arg_keys[9], N_EP)).reshape((N_EP, REQ_DEV)).astype(jnp.int32)
    final_gain = jnp.clip(1.0 + 0.15 * jax.random.normal(arg_keys[10], (D,), jnp.float32), 0.25, 1.75)
    head = bell_draw(arg_keys[11], (VOCAB, D), (D // 16) ** -0.5, 0.375, ((0, 512),))
    return {"attn": attn, "resid": resid, "wo": wo, "norm_gain": norm_gain, "router": router, "expert_ids": expert_ids, "w_gate": w_gate, "w_up": w_up, "w_down": w_down, "lengths": lengths, "final_gain": final_gain, "head": head}


def rms_scale(values, gain):
    return values * lax.rsqrt(lax.optimization_barrier(jnp.mean(values * values, axis=1, keepdims=True)) + 1e-05) * gain

def reference(attn, resid, wo, norm_gain, router, expert_ids, w_gate, w_up, w_down, lengths, final_gain, head):
    proj = jnp.dot(attn, wo, preferred_element_type=jnp.float32)
    stream = resid.astype(jnp.float32) + proj
    normed = rms_scale(stream, norm_gain).astype(jnp.bfloat16)
    logits = jnp.dot(normed, router, preferred_element_type=jnp.float32)
    picked = jnp.take_along_axis(logits, expert_ids, axis=1)
    first = 1.0 / (1.0 + jnp.exp(picked[:, 1] - picked[:, 0]))
    second = 1.0 / (1.0 + jnp.exp(picked[:, 0] - picked[:, 1]))
    both_weights = jnp.stack([first, second], axis=1)
    slots = N_EP * CAP
    blocks = FF // FF_DEV
    total = stream
    for expert in range(EXPERTS):
        chosen = expert_ids == expert
        weight = lax.optimization_barrier(jnp.sum(jnp.where(chosen, both_weights, 0.0), axis=1))
        member = jnp.any(chosen, axis=1)
        count = jnp.sum(member.astype(jnp.int32))
        index = jnp.nonzero(member, size=slots, fill_value=0)[0].astype(jnp.int32)
        picked_rows = normed[index]
        gate = jnp.dot(picked_rows, w_gate[:, expert * FF:(expert + 1) * FF], preferred_element_type=jnp.float32)
        upper = jnp.dot(picked_rows, w_up[:, expert * FF:(expert + 1) * FF], preferred_element_type=jnp.float32)
        hidden = (jax.nn.silu(gate) * upper).astype(jnp.bfloat16)
        hidden_blocks = hidden.reshape(slots, blocks, FF_DEV).transpose(1, 0, 2)
        down_blocks = w_down[expert * FF:(expert + 1) * FF].reshape(blocks, FF_DEV, D)

        def add_block(carry, pair):
            term = jnp.dot(pair[0], pair[1], preferred_element_type=jnp.float32).astype(jnp.bfloat16)
            term = lax.optimization_barrier(term)
            return (carry + term.astype(jnp.float32), None)
        expert_out, _ = lax.scan(add_block, jnp.zeros((slots, D), jnp.float32), (hidden_blocks, down_blocks))
        valid = jnp.arange(slots, dtype=jnp.int32) < count
        coef = jnp.where(valid, weight[index], 0.0)
        total = total.at[index].add(expert_out * coef[:, None])
    mixed = total.astype(jnp.bfloat16)
    offsets = (jnp.arange(N_EP, dtype=jnp.int32) * ROWS)[:, None]
    ends = (jnp.cumsum(lengths, axis=1).astype(jnp.int32) - 1 + offsets).reshape(-1)
    last = mixed[ends].astype(jnp.float32)
    final = rms_scale(last, final_gain).astype(jnp.bfloat16)
    vocab_logits = jnp.dot(final, head.T, preferred_element_type=jnp.float32)
    max_logit = lax.optimization_barrier(jnp.max(vocab_logits, axis=1))
    return (mixed, max_logit)
```

```python
import jax
import jax.numpy as jnp
from jax import lax
from jax.experimental import pallas as pl
from jax.experimental.pallas import tpu as pltpu
from jax.sharding import PartitionSpec as P

F32 = jnp.float32
BF16 = jnp.bfloat16
NX, NY, NZ, NQ = 4, 8, 8, 32
MESH = pl.DeviceIdType.MESH
LOW = -3.0e38


def iota(shape, axis):
    return lax.broadcasted_iota(jnp.int32, shape, axis)


def mm(a, b):
    return jnp.dot(a, b, preferred_element_type=F32)


def near(i, t):
    half = (i + 1) // 2
    return (t + half * (2 * (i % 2) - 1) + NZ) % NZ


def kernel(
    attn, resid, wo, gain, router, ids, w_gate, w_up, w_down, lengths, final_gain, head,
    mixed, best,
    wo2, wg2, wu2, wd2, hd,
    at, p3, pb, pr, sb, xb, x32, eb, rb,
    db, yd, g, acc, tb, xr, zb, zr, yb, yr, mx, fr, lpb, rl, mq, mz,
    send, recv, gz, gx, tx, bg_send, bg_recv, bg_local,
):
    ep = lax.axis_index("ep")
    t = lax.axis_index("tp")
    q = ep // 2
    c = ep % 2
    y = q // NX
    x = q % NX

    def at_q(k):
        return (2 * k + c, t)

    def at_z(k):
        return (ep, k)

    def at_y(k):
        return ((k * NX + x) * 2 + c, t)

    def at_x(k):
        return ((y * NX + k) * 2 + c, t)

    def at_cz(k):
        return (2 * q + k // NZ, k % NZ)

    other = (2 * q + 1 - c, t)
    mine_cz = c * NZ + t

    def each(count, me, body):
        def step(d, carry):
            body((me + d) % count)
            return carry

        lax.fori_loop(1, count, step, 0)

    def push(src, dst, where, send_sem, recv_sem):
        pltpu.make_async_remote_copy(
            src_ref=src, dst_ref=dst, send_sem=send_sem, recv_sem=recv_sem,
            device_id=where, device_id_type=MESH,
        ).start()

    def drain(ref, sem):
        pltpu.make_async_copy(ref, ref, sem).wait()

    barrier = pltpu.get_barrier_semaphore()

    def hello(where):
        pl.semaphore_signal(barrier, inc=1, device_id=where, device_id_type=MESH)

    each(NQ, q, lambda k: hello(at_q(k)))
    each(2 * NZ, mine_cz, lambda k: hello(at_cz(k)))
    at[q] = attn[...]
    pl.semaphore_wait(barrier, NQ - 1 + 2 * NZ - 1)

    each(NQ, q, lambda k: push(at.at[q], at.at[q], at_q(k), send.at[0], recv.at[0]))

    pairs = ((wo, wo2), (w_gate, wg2), (w_up, wu2), (w_down, wd2))
    for n, (src, dst) in enumerate(pairs):
        push(src, dst.at[c], other, bg_send.at[n], bg_recv.at[n])
        pltpu.make_async_copy(src, dst.at[c], bg_local.at[n]).start()

    def head_part(k):
        return head.at[:, pl.ds(pl.multiple_of((k % NZ) * 512, 512), 512)]

    each(2 * NZ, mine_cz, lambda k: push(
        head_part(k), hd.at[mine_cz], at_cz(k), bg_send.at[4], bg_recv.at[4]))
    pltpu.make_async_copy(head_part(t), hd.at[mine_cz], bg_local.at[4]).start()

    rows = resid[...].astype(F32)
    row = jnp.sum(jnp.where(iota(rows.shape, 0) == t, rows, 0.0), axis=0, keepdims=True)
    for k in range(NQ):
        x32[k:k + 1, :] = row[:, 128 * k:128 * k + 128]

    id0 = ids[:, 0:1]
    id1 = ids[:, 1:2]
    id0_32 = jnp.concatenate([id0] * 4, axis=0)
    id1_32 = jnp.concatenate([id1] * 4, axis=0)
    r_i = iota((32, 128), 0)
    c_i = iota((32, 128), 1)
    col_k = c_i >> 4
    is0 = id0_32 == col_k
    is1 = id1_32 == col_k
    member = jnp.where(is0 | is1, 1.0, 0.0)
    lr = iota((32, 32), 0)
    lc = iota((32, 32), 1)
    lower = jnp.where(((lr >> 3) == (lc >> 3)) & (lc < lr), 1.0, 0.0)
    earlier = mm(lower.astype(BF16), member.astype(BF16))
    slot = (c_i & 3).astype(F32)
    placed = jnp.where(
        (jnp.abs(earlier - slot) < 0.5) & ((r_i >> 3) == ((c_i >> 2) & 3)), member, 0.0)
    ra = iota((128, 128), 0)
    ca = iota((128, 128), 1)
    perm = jnp.where(ca == 16 * ((ra >> 2) & 7) + 4 * (ra >> 5) + (ra & 3), 1.0, 0.0).astype(BF16)
    perm_t = jnp.where(ra == 16 * ((ca >> 2) & 7) + 4 * (ca >> 5) + (ca & 3), 1.0, 0.0).astype(BF16)

    for n in range(1):
        drain(wo2.at[1 - c], bg_recv.at[n])
        drain(wo2.at[c], bg_local.at[n])
    drain(at.at[pl.ds(0, NQ - 1)], recv.at[0])
    a = at[...].astype(F32).reshape(256, 512).astype(BF16)
    part = jnp.concatenate([mm(a, wo2[0]), mm(a, wo2[1])], axis=1)
    p3[...] = part.reshape(NQ, 8, 128)
    for r in range(NZ):
        pb[r] = p3[:, r, :]
    each(NZ, t, lambda k: push(pb.at[k], pr.at[t], at_z(k), send.at[1], recv.at[1]))
    pr[t] = pb[t]
    drain(pr.at[pl.ds(0, NZ - 1)], recv.at[1])
    sb[:, 0, :] = jnp.sum(pr[...], axis=0)
    each(NQ, q, lambda k: push(sb.at[k], xb.at[q], at_q(k), send.at[2], recv.at[2]))
    xb[q] = sb[q]
    drain(xb.at[pl.ds(0, NQ - 1)], recv.at[2])

    xrow = x32[...] + xb[:, 0, :]
    x32[...] = xrow
    scale = lax.rsqrt(jnp.sum(xrow * xrow, keepdims=True) * (1.0 / 4096) + 1e-05)
    hrow = (xrow * scale * gain[...]).astype(BF16).astype(F32)
    lane = iota((1, 128), 1)
    stats = jnp.where(lane == 0, scale, 0.0)
    for k in range(8):
        one = jnp.sum(hrow * router[k].astype(F32), keepdims=True)
        stats = stats + jnp.where(lane == 8 + k, one, 0.0)
    eb[...] = jnp.zeros_like(eb)
    for k in range(NZ):
        eb[k, 0:4, :] = x32[4 * k:4 * k + 4, :]
        eb[k, 4:5, :] = stats
    each(NZ, t, lambda k: push(eb.at[k], rb.at[t], at_z(k), send.at[3], recv.at[3]))
    rb[t] = eb[t]
    drain(rb.at[pl.ds(0, NZ - 1)], recv.at[3])

    xs = jnp.concatenate([rb[:, j, :] for j in range(4)], axis=0)
    st = rb[:, 4, :]
    scale32 = jnp.concatenate([st[:, 0:1]] * 4, axis=0)
    gain32 = jnp.concatenate(
        [jnp.broadcast_to(gain[pl.ds(4 * t + j, 1), :], (8, 128)) for j in range(4)], axis=0)
    fgain32 = jnp.concatenate(
        [jnp.broadcast_to(final_gain[pl.ds(4 * t + j, 1), :], (8, 128)) for j in range(4)], axis=0)
    h32 = (xs * scale32 * gain32).astype(BF16)
    lane8 = iota((8, 128), 1)
    la = jnp.sum(jnp.where(lane8 == id0 + 8, st, 0.0), axis=1, keepdims=True)
    lb = jnp.sum(jnp.where(lane8 == id1 + 8, st, 0.0), axis=1, keepdims=True)
    wa = 1.0 / (1.0 + jnp.exp(lb - la))
    wb = 1.0 / (1.0 + jnp.exp(la - lb))
    wa32 = jnp.concatenate([wa] * 4, axis=0)
    wb32 = jnp.concatenate([wb] * 4, axis=0)
    combine = placed * jnp.where(is0, wa32, wb32)

    disp = lax.dot_general(
        placed.astype(BF16), h32, (((0,), (0,)), ((), ())), preferred_element_type=F32)
    db[...] = disp.astype(BF16).reshape(NY, 16, 128)
    each(NY, y, lambda k: push(db.at[k], yd.at[y], at_y(k), send.at[4], recv.at[4]))
    yd[y] = db[y]
    drain(yd.at[pl.ds(0, NY - 1)], recv.at[4])
    slots = mm(perm, yd[...].reshape(128, 128)).astype(BF16)
    for j in range(4):
        g[x, t, :, 128 * j:128 * j + 128] = slots[32 * j:32 * j + 32, :]
    each(NZ, t, lambda k: push(g.at[x, t], g.at[x, t], at_z(k), send.at[5], gz.at[t]))
    each(NX, x, lambda k: push(g.at[x, t], g.at[x, t], at_x(k), send.at[6], gx.at[t]))

    def forward(i, carry):
        z = near(i, t)
        drain(g.at[x, z], gz.at[z])
        each(NX, x, lambda k: push(g.at[x, z], g.at[x, z], at_x(k), send.at[6], gx.at[z]))
        return carry

    lax.fori_loop(1, NZ, forward, 0)

    for n in (1, 2, 3):
        dst = pairs[n][1]
        drain(dst.at[1 - c], bg_recv.at[n])
        drain(dst.at[c], bg_local.at[n])
    acc[...] = jnp.zeros_like(acc)

    def up_step(i, carry):
        z = near(i, t)
        drain(g.at[pl.ds(0, NX - 1), z], gx.at[z])
        lhs = g[:, z].reshape(128, 512)
        start = pl.multiple_of(z * 512, 512)
        for k in range(2):
            acc[k] += mm(lhs, wg2[k, pl.ds(start, 512), :])
            acc[2 + k] += mm(lhs, wu2[k, pl.ds(start, 512), :])
        return carry

    lax.fori_loop(0, NZ, up_step, 0)
    hidden = jnp.concatenate(
        [acc[k] * jax.nn.sigmoid(acc[k]) * acc[2 + k] for k in range(2)], axis=1).astype(BF16)

    def down_step(i, carry):
        z = near(NZ - 1 - i, t)
        start = pl.multiple_of(z * 512, 512)
        term = mm(hidden, wd2[:, :, pl.ds(start, 512)].reshape(256, 512))
        tb[:, z] = term.reshape(NX, 32, 512).astype(BF16)
        each(NX, x, lambda k: push(tb.at[k, z], xr.at[x, z], at_x(k), send.at[7], tx.at[z]))
        xr[x, z] = tb[x, z]
        return carry

    lax.fori_loop(0, NZ, down_step, 0)

    def sum_x(z):
        drain(xr.at[pl.ds(0, NX - 1), z], tx.at[z])
        return jnp.sum(xr[:, z].astype(F32), axis=0).astype(BF16)

    def sum_step(i, carry):
        z = near(NZ - 1 - i, t)
        zb[z] = sum_x(z)
        push(zb.at[z], zr.at[t], at_z(z), send.at[8], recv.at[8])
        return carry

    lax.fori_loop(0, NZ - 1, sum_step, 0)
    zr[t] = sum_x(t)
    drain(zr.at[pl.ds(0, NZ - 1)], recv.at[8])
    total = jnp.sum(zr[...].astype(F32), axis=0)
    stacked = jnp.concatenate(
        [total[:, 128 * j:128 * j + 128] for j in range(4)], axis=0).astype(BF16)
    yb[...] = mm(perm_t, stacked).astype(BF16).reshape(NY, 16, 128)
    each(NY, y, lambda k: push(yb.at[k], yr.at[y], at_y(k), send.at[9], recv.at[9]))
    yr[y] = yb[y]
    drain(yr.at[pl.ds(0, NY - 1)], recv.at[9])

    back = yr[...].reshape(128, 128).astype(F32)
    out32 = jnp.dot(combine, back, precision=lax.Precision.HIGHEST, preferred_element_type=F32)
    mx[t] = (xs + out32).astype(BF16)
    each(NZ, t, lambda k: push(mx.at[t], mx.at[t], at_z(k), send.at[10], recv.at[10]))
    drain(mx.at[pl.ds(0, NZ - 1)], recv.at[10])
    m3 = mx[...].astype(F32)
    mixed[...] = jnp.concatenate(
        [m3[z, 8 * j:8 * j + 8, :] for z in range(NZ) for j in range(4)], axis=1).astype(BF16)

    ss = jnp.sum(jnp.sum(m3 * m3, axis=0), axis=1, keepdims=True)
    ss8 = ss[0:8] + ss[8:16] + ss[16:24] + ss[24:32]
    scale2 = lax.rsqrt(ss8 * (1.0 / 4096) + 1e-05)
    own = mx[t].astype(F32)
    fin = (own * jnp.concatenate([scale2] * 4, axis=0) * fgain32).astype(BF16)
    lens = jnp.broadcast_to(lengths[...], (16, 4))
    ends = jnp.sum(
        jnp.where(iota((16, 4), 1) <= (iota((16, 4), 0) & 3), lens, 0), axis=1, keepdims=True) - 1
    sr = iota((16, 32), 0)
    sc = iota((16, 32), 1)
    pick = jnp.where(((sr >> 2) == (sc >> 3)) & (ends == (sc & 7)), 1.0, 0.0).astype(BF16)
    fr[q] = mm(pick, fin).astype(BF16)
    each(NQ, q, lambda k: push(fr.at[q], fr.at[q], at_q(k), send.at[11], recv.at[11]))
    drain(hd.at[pl.ds(0, 2 * NZ - 1)], bg_recv.at[4])
    drain(hd.at[0], bg_local.at[4])
    drain(fr.at[pl.ds(0, NQ - 1)], recv.at[11])

    rows512 = fr[...].reshape(512, 128)
    vocab = hd[...].reshape(512, 512)
    fa = iota((128, 512), 0)
    fb = iota((128, 512), 1)
    logits = jnp.zeros((128, 512), F32)
    for j in range(4):
        order = jnp.where(fb == 16 * (fa >> 2) + 4 * j + (fa & 3), 1.0, 0.0).astype(BF16)
        rows_j = mm(order, rows512).astype(BF16)
        logits = logits + lax.dot_general(
            rows_j, vocab[:, 128 * j:128 * j + 128], (((1,), (1,)), ((), ())),
            preferred_element_type=F32)
    lpb[...] = logits.reshape(NZ, 16, 512)
    each(NZ, t, lambda k: push(lpb.at[k], rl.at[t], at_z(k), send.at[12], recv.at[12]))
    rl[t] = lpb[t]
    drain(rl.at[pl.ds(0, NZ - 1)], recv.at[12])
    top = jnp.max(jnp.sum(rl[...], axis=0), axis=1, keepdims=True)
    spread = jnp.where(iota((16, 128), 1) == iota((16, 128), 0) + 16 * t, top, LOW)
    mq[q] = jnp.max(spread, axis=0, keepdims=True)
    each(NQ, q, lambda k: push(mq.at[q], mq.at[q], at_q(k), send.at[13], recv.at[13]))
    drain(mq.at[pl.ds(0, NQ - 1)], recv.at[13])
    mz[mine_cz] = jnp.max(mq[:, 0, :], axis=0, keepdims=True)
    each(2 * NZ, mine_cz, lambda k: push(
        mz.at[mine_cz], mz.at[mine_cz], at_cz(k), send.at[14], recv.at[14]))
    drain(mz.at[pl.ds(0, 2 * NZ - 1)], recv.at[14])
    both = mz[:, 0, :]
    best[0:1, :] = jnp.max(both[0:8], axis=0, keepdims=True)
    best[1:2, :] = jnp.max(both[8:16], axis=0, keepdims=True)

    for n, (src, dst) in enumerate(pairs):
        drain(dst.at[c], bg_send.at[n])
    drain(hd.at[pl.ds(0, 2 * NZ - 1)], bg_send.at[4])
    sent = (
        at.at[pl.ds(0, NQ - 1)], pb.at[pl.ds(0, NZ - 1)], sb.at[pl.ds(0, NQ - 1)],
        eb.at[pl.ds(0, NZ - 1)], db.at[pl.ds(0, NY - 1)], g.at[0, pl.ds(0, NZ - 1)],
        g.at[pl.ds(0, NX - 1)], tb.at[pl.ds(0, NX - 1)], zb.at[pl.ds(0, NZ - 1)],
        yb.at[pl.ds(0, NY - 1)], mx.at[pl.ds(0, NZ - 1)], fr.at[pl.ds(0, NQ - 1)],
        lpb.at[pl.ds(0, NZ - 1)], mq.at[pl.ds(0, NQ - 1)], mz.at[pl.ds(0, 2 * NZ - 1)],
    )
    for n, ref in enumerate(sent):
        drain(ref, send.at[n])


def local(
    attn, resid, wo, norm_gain, router, expert_ids, w_gate, w_up, w_down, lengths, final_gain, head
):
    vm = pl.BlockSpec(memory_space=pltpu.VMEM)
    hbm = pl.BlockSpec(memory_space=pl.ANY)
    v = pltpu.VMEM
    dma = pltpu.SemaphoreType.DMA
    mixed, best = pl.pallas_call(
        kernel,
        out_shape=(
            jax.ShapeDtypeStruct((8, 4096), BF16),
            jax.ShapeDtypeStruct((2, 128), F32),
        ),
        in_specs=[vm, vm, hbm, vm, vm, vm, hbm, hbm, hbm, vm, vm, hbm],
        out_specs=(vm, vm),
        scratch_shapes=[
            v((2, 512, 64), BF16), v((2, 4096, 128), BF16), v((2, 4096, 128), BF16),
            v((2, 128, 4096), BF16), v((16, 32, 512), BF16),
            v((NQ, 8, 512), BF16), v((NQ, 8, 128), F32), v((NZ, NQ, 128), F32),
            v((NZ, NQ, 128), F32), v((NQ, 1, 128), F32), v((NQ, 1, 128), F32),
            v((NQ, 128), F32), v((NZ, 8, 128), F32), v((NZ, 8, 128), F32),
            v((NY, 16, 128), BF16), v((NY, 16, 128), BF16), v((NX, NZ, 32, 512), BF16),
            v((4, 128, 128), F32), v((NX, NZ, 32, 512), BF16), v((NX, NZ, 32, 512), BF16),
            v((NZ, 32, 512), BF16), v((NZ, 32, 512), BF16), v((NY, 16, 128), BF16),
            v((NY, 16, 128), BF16), v((NZ, 32, 128), BF16), v((NQ, 16, 128), BF16),
            v((NZ, 16, 512), F32), v((NZ, 16, 512), F32), v((NQ, 1, 128), F32),
            v((2 * NZ, 1, 128), F32),
            dma((15,)), dma((15,)), dma((NZ,)), dma((NZ,)), dma((NZ,)),
            dma((5,)), dma((5,)), dma((5,)),
        ],
        compiler_params=pltpu.CompilerParams(
            collective_id=0, has_side_effects=True, vmem_limit_bytes=48 << 20),
    )(
        attn, resid, wo, norm_gain.reshape(NQ, 128), router.T.reshape(8, NQ, 128), expert_ids,
        w_gate, w_up, w_down, lengths, final_gain.reshape(NQ, 128), head,
    )
    max_logit = best.reshape(2, NQ, 4).transpose(1, 0, 2).reshape(256)
    return mixed, max_logit


def solution(mesh):
    placed = (
        P("ep", "tp"),
        P("ep", None),
        P("tp", "ep"),
        P(),
        P(),
        P("ep", None),
        P(None, ("ep", "tp")),
        P(None, ("ep", "tp")),
        P(("ep", "tp"), None),
        P("ep", None),
        P(),
        P(("ep", "tp"), None),
    )
    return jax.shard_map(
        local, mesh=mesh, in_specs=placed, out_specs=(P("ep", None), P()), check_vma=False
    )
```

```python
import jax
import jax.numpy as jnp
from jax import lax
from jax.experimental import pallas as pl
from jax.experimental.pallas import tpu as pltpu
from jax.sharding import PartitionSpec as P

F32 = jnp.float32
BF16 = jnp.bfloat16
NX, NY, NZ, NQ = 4, 8, 8, 32
MESH = pl.DeviceIdType.MESH
LOW = -3.0e38


def iota(shape, axis):
    return lax.broadcasted_iota(jnp.int32, shape, axis)


def mm(a, b):
    return jnp.dot(a, b, preferred_element_type=F32)


def near(i, t):
    half = (i + 1) // 2
    return (t + half * (2 * (i % 2) - 1) + NZ) % NZ


def kernel(
    attn, resid_in, wo, gain_in, router_in, ids_in, w_gate, w_up, w_down, lengths_in, fgain_in,
    head,
    mixed, best,
    resid, gain, router, ids, lengths, final_gain, wo2, wg2, wu2, wd2, hd,
    at, p3, pb, pr, sb, xb, x32, eb, rb,
    db, yd, g, acc, tb, xr, zb, zr, yb, yr, mx, fr, lpb, rl, mq, mz, order,
    send, recv, gz, gx, tx, bg_send, bg_recv, bg_local, small,
):
    ep = lax.axis_index("ep")
    t = lax.axis_index("tp")
    q = ep // 2
    c = ep % 2
    y = q // NX
    x = q % NX

    def at_q(k):
        return (2 * k + c, t)

    def at_z(k):
        return (ep, k)

    def at_y(k):
        return ((k * NX + x) * 2 + c, t)

    def at_x(k):
        return ((y * NX + k) * 2 + c, t)

    def at_cz(k):
        return (2 * q + k // NZ, k % NZ)

    other = (2 * q + 1 - c, t)
    mine_cz = c * NZ + t

    def each(count, me, body):
        def step(d, carry):
            body((me + d) % count)
            return carry

        lax.fori_loop(1, count, step, 0)

    def push(src, dst, where, send_sem, recv_sem):
        pltpu.make_async_remote_copy(
            src_ref=src, dst_ref=dst, send_sem=send_sem, recv_sem=recv_sem,
            device_id=where, device_id_type=MESH,
        ).start()

    def drain(ref, sem):
        pltpu.make_async_copy(ref, ref, sem).wait()

    inputs = (
        (attn, at.at[q]), (resid_in, resid), (gain_in, gain), (router_in, router),
        (ids_in, ids), (lengths_in, lengths), (fgain_in, final_gain),
    )
    for n, (src, dst) in enumerate(inputs):
        pltpu.make_async_copy(src, dst, small.at[n]).start()

    barrier = pltpu.get_barrier_semaphore()

    def hello(where):
        pl.semaphore_signal(barrier, inc=1, device_id=where, device_id_type=MESH)

    each(NQ, q, lambda k: hello(at_q(k)))
    each(2 * NZ, mine_cz, lambda k: hello(at_cz(k)))
    drain(at.at[q], small.at[0])
    pl.semaphore_wait(barrier, NQ - 1 + 2 * NZ - 1)

    each(NQ, q, lambda k: push(at.at[q], at.at[q], at_q(k), send.at[0], recv.at[0]))

    pairs = ((wo, wo2), (w_gate, wg2), (w_up, wu2), (w_down, wd2))

    def swap(n):
        src, dst = pairs[n]
        push(src, dst.at[c], other, bg_send.at[n], bg_recv.at[n])
        pltpu.make_async_copy(src, dst.at[c], bg_local.at[n]).start()

    swap(0)

    def head_part(k):
        return head.at[:, pl.ds(pl.multiple_of((k % NZ) * 512, 512), 512)]

    for n in range(1, len(inputs)):
        drain(inputs[n][1], small.at[n])

    rows = resid[...].astype(F32)
    row = jnp.sum(jnp.where(iota(rows.shape, 0) == t, rows, 0.0), axis=0, keepdims=True)
    for k in range(NQ):
        x32[k:k + 1, :] = row[:, 128 * k:128 * k + 128]

    eye = iota((8, 8), 0) == iota((8, 8), 1)
    id0 = jnp.sum(jnp.where(eye, ids[0:1, :], 0), axis=1, keepdims=True)
    id1 = jnp.sum(jnp.where(eye, ids[1:2, :], 0), axis=1, keepdims=True)
    id0_32 = jnp.concatenate([id0] * 4, axis=0)
    id1_32 = jnp.concatenate([id1] * 4, axis=0)
    r_i = iota((32, 128), 0)
    c_i = iota((32, 128), 1)
    col_k = c_i >> 4
    is0 = id0_32 == col_k
    is1 = id1_32 == col_k
    member = jnp.where(is0 | is1, 1.0, 0.0)
    lr = iota((32, 32), 0)
    lc = iota((32, 32), 1)
    lower = jnp.where(((lr >> 3) == (lc >> 3)) & (lc < lr), 1.0, 0.0)
    earlier = mm(lower.astype(BF16), member.astype(BF16))
    slot = (c_i & 3).astype(F32)
    placed = jnp.where(
        (jnp.abs(earlier - slot) < 0.5) & ((r_i >> 3) == ((c_i >> 2) & 3)), member, 0.0)
    ra = iota((128, 128), 0)
    ca = iota((128, 128), 1)
    perm = jnp.where(ca == 16 * ((ra >> 2) & 7) + 4 * (ra >> 5) + (ra & 3), 1.0, 0.0).astype(BF16)
    perm_t = jnp.where(ra == 16 * ((ca >> 2) & 7) + 4 * (ca >> 5) + (ca & 3), 1.0, 0.0).astype(BF16)

    lens = jnp.broadcast_to(lengths[...], (16, 4))
    ends = jnp.sum(
        jnp.where(iota((16, 4), 1) <= (iota((16, 4), 0) & 3), lens, 0), axis=1, keepdims=True) - 1
    sr = iota((16, 32), 0)
    sc = iota((16, 32), 1)
    pick = jnp.where(((sr >> 2) == (sc >> 3)) & (ends == (sc & 7)), 1.0, 0.0).astype(BF16)
    fa = iota((128, 512), 0)
    fb = iota((128, 512), 1) - 16 * (fa >> 2) - (fa & 3)
    for j in range(4):
        order[j] = jnp.where(fb == 4 * j, 1.0, 0.0).astype(BF16)

    drain(wo2.at[1 - c], bg_recv.at[0])
    drain(wo2.at[c], bg_local.at[0])
    drain(at.at[pl.ds(0, NQ - 1)], recv.at[0])
    for n in (1, 2, 3):
        swap(n)
    a = at[...].astype(F32).reshape(256, 512).astype(BF16)
    part = lax.dot_general(
        a, wo2[...].reshape(128, 512), (((1,), (1,)), ((), ())), preferred_element_type=F32)
    p3[...] = part.reshape(NQ, 8, 128)
    for r in range(NZ):
        pb[r] = p3[:, r, :]
    each(NZ, t, lambda k: push(pb.at[k], pr.at[t], at_z(k), send.at[1], recv.at[1]))
    pr[t] = pb[t]
    drain(pr.at[pl.ds(0, NZ - 1)], recv.at[1])
    sb[:, 0, :] = jnp.sum(pr[...], axis=0)
    each(NQ, q, lambda k: push(sb.at[k], xb.at[q], at_q(k), send.at[2], recv.at[2]))
    xb[q] = sb[q]
    drain(xb.at[pl.ds(0, NQ - 1)], recv.at[2])

    xrow = x32[...] + xb[:, 0, :]
    scale = lax.rsqrt(jnp.sum(xrow * xrow, keepdims=True) * (1.0 / 4096) + 1e-05)
    hrow = (xrow * scale * gain[...]).astype(BF16).astype(F32)
    lane = iota((1, 128), 1)
    x32[...] = hrow
    dots = jnp.zeros((8, 128), F32)
    for k in range(NQ):
        dots = dots + x32[k:k + 1, :] * router[:, 128 * k:128 * k + 128].astype(F32)
    x32[...] = xrow
    dots = jnp.sum(dots, axis=1, keepdims=True)
    put = jnp.where(iota((8, 128), 1) == iota((8, 128), 0) + 8, dots, 0.0)
    stats = jnp.where(lane == 0, scale, 0.0) + jnp.sum(put, axis=0, keepdims=True)
    eb[...] = jnp.zeros_like(eb)
    for k in range(NZ):
        eb[k, 0:4, :] = x32[4 * k:4 * k + 4, :]
        eb[k, 4:5, :] = stats
    each(NZ, t, lambda k: push(eb.at[k], rb.at[t], at_z(k), send.at[3], recv.at[3]))
    rb[t] = eb[t]
    drain(rb.at[pl.ds(0, NZ - 1)], recv.at[3])

    xs = jnp.concatenate([rb[:, j, :] for j in range(4)], axis=0)
    st = rb[:, 4, :]
    scale32 = jnp.concatenate([st[:, 0:1]] * 4, axis=0)
    gain32 = jnp.concatenate(
        [jnp.broadcast_to(gain[pl.ds(4 * t + j, 1), :], (8, 128)) for j in range(4)], axis=0)
    h32 = (xs * scale32 * gain32).astype(BF16)
    lane8 = iota((8, 128), 1)
    la = jnp.sum(jnp.where(lane8 == id0 + 8, st, 0.0), axis=1, keepdims=True)
    lb = jnp.sum(jnp.where(lane8 == id1 + 8, st, 0.0), axis=1, keepdims=True)
    wa = 1.0 / (1.0 + jnp.exp(lb - la))
    wb = 1.0 / (1.0 + jnp.exp(la - lb))
    wa32 = jnp.concatenate([wa] * 4, axis=0)
    wb32 = jnp.concatenate([wb] * 4, axis=0)
    combine = placed * jnp.where(is0, wa32, wb32)

    each(NZ, t, lambda k: push(
        head_part(k), hd.at[mine_cz], at_z(k), bg_send.at[4], bg_recv.at[4]))
    pltpu.make_async_copy(head_part(t), hd.at[mine_cz], bg_local.at[4]).start()

    disp = lax.dot_general(
        placed.astype(BF16), h32, (((0,), (0,)), ((), ())), preferred_element_type=F32)
    db[...] = disp.astype(BF16).reshape(NY, 16, 128)
    each(NY, y, lambda k: push(db.at[k], yd.at[y], at_y(k), send.at[4], recv.at[4]))
    yd[y] = db[y]
    drain(yd.at[pl.ds(0, NY - 1)], recv.at[4])
    slots = mm(perm, yd[...].reshape(128, 128)).astype(BF16)
    for j in range(4):
        g[x, t, :, 128 * j:128 * j + 128] = slots[32 * j:32 * j + 32, :]
    each(NZ, t, lambda k: push(g.at[x, t], g.at[x, t], at_z(k), send.at[5], gz.at[t]))
    each(NX, x, lambda k: push(g.at[x, t], g.at[x, t], at_x(k), send.at[6], gx.at[t]))

    def forward(i, carry):
        z = near(i, t)
        drain(g.at[x, z], gz.at[z])
        each(NX, x, lambda k: push(g.at[x, z], g.at[x, z], at_x(k), send.at[6], gx.at[z]))
        return carry

    lax.fori_loop(1, NZ, forward, 0)

    for n in (1, 2, 3):
        dst = pairs[n][1]
        drain(dst.at[1 - c], bg_recv.at[n])
        drain(dst.at[c], bg_local.at[n])
    acc[...] = jnp.zeros_like(acc)

    def up_step(i, carry):
        z = near(i, t)
        drain(g.at[pl.ds(0, NX - 1), z], gx.at[z])
        lhs = g[:, z].reshape(128, 512)
        start = pl.multiple_of(z * 512, 512)
        for k in range(2):
            acc[k] += mm(lhs, wg2[k, pl.ds(start, 512), :])
            acc[2 + k] += mm(lhs, wu2[k, pl.ds(start, 512), :])
        return carry

    lax.fori_loop(0, NZ, up_step, 0)
    hidden = jnp.concatenate(
        [acc[k] * jax.nn.sigmoid(acc[k]) * acc[2 + k] for k in range(2)], axis=1).astype(BF16)

    def down_step(i, carry):
        z = near(NZ - 1 - i, t)
        start = pl.multiple_of(z * 512, 512)
        term = mm(hidden, wd2[:, :, pl.ds(start, 512)].reshape(256, 512))
        tb[:, z] = term.reshape(NX, 32, 512).astype(BF16)
        each(NX, x, lambda k: push(tb.at[k, z], xr.at[x, z], at_x(k), send.at[7], tx.at[z]))
        xr[x, z] = tb[x, z]
        return carry

    lax.fori_loop(0, NZ, down_step, 0)

    def sum_x(z):
        drain(xr.at[pl.ds(0, NX - 1), z], tx.at[z])
        return jnp.sum(xr[:, z].astype(F32), axis=0).astype(BF16)

    def sum_step(i, carry):
        z = near(NZ - 1 - i, t)
        zb[z] = sum_x(z)
        push(zb.at[z], zr.at[t], at_z(z), send.at[8], recv.at[8])
        return carry

    lax.fori_loop(0, NZ - 1, sum_step, 0)
    zr[t] = sum_x(t)
    drain(zr.at[pl.ds(0, NZ - 1)], recv.at[8])
    total = jnp.sum(zr[...].astype(F32), axis=0)
    stacked = jnp.concatenate(
        [total[:, 128 * j:128 * j + 128] for j in range(4)], axis=0).astype(BF16)
    yb[...] = mm(perm_t, stacked).astype(BF16).reshape(NY, 16, 128)
    each(NY, y, lambda k: push(yb.at[k], yr.at[y], at_y(k), send.at[9], recv.at[9]))
    yr[y] = yb[y]
    drain(yr.at[pl.ds(0, NY - 1)], recv.at[9])

    mine = hd.at[pl.ds(c * NZ, NZ)]
    drain(hd.at[pl.ds(0, NZ - 1)], bg_recv.at[4])
    drain(hd.at[0], bg_local.at[4])
    push(mine, mine, other, bg_send.at[5], bg_recv.at[5])

    back = yr[...].reshape(128, 128).astype(F32)
    out32 = jnp.dot(combine, back, precision=lax.Precision.HIGHEST, preferred_element_type=F32)
    own = (xs + out32).astype(BF16)
    mx[t] = own
    fr[q] = mm(pick, own).astype(BF16)
    each(NQ, q, lambda k: push(fr.at[q], fr.at[q], at_q(k), send.at[11], recv.at[11]))
    each(NZ, t, lambda k: push(mx.at[t], mx.at[t], at_z(k), send.at[10], recv.at[10]))
    drain(mine, bg_recv.at[5])
    drain(fr.at[pl.ds(0, NQ - 1)], recv.at[11])

    rows512 = fr[...].reshape(512, 128)
    vocab = hd[...].reshape(512, 512)
    logits = jnp.zeros((128, 512), F32)
    squares = jnp.zeros((128, 128), F32)
    for j in range(4):
        rows_j = mm(order[j], rows512)
        squares = squares + rows_j * rows_j
        fin = (rows_j * final_gain[pl.ds(4 * t + j, 1), :]).astype(BF16)
        logits = logits + lax.dot_general(
            fin, vocab[:, 128 * j:128 * j + 128], (((1,), (1,)), ((), ())),
            preferred_element_type=F32)
    squares = jnp.broadcast_to(jnp.sum(squares, axis=1, keepdims=True), (128, 128))
    lpb[:, :, 0:512] = logits.reshape(NZ, 16, 512)
    lpb[:, :, 512:640] = squares.reshape(NZ, 16, 128)
    each(NZ, t, lambda k: push(lpb.at[k], rl.at[t], at_z(k), send.at[12], recv.at[12]))
    rl[t] = lpb[t]
    drain(mx.at[pl.ds(0, NZ - 1)], recv.at[10])
    m3 = mx[...].astype(F32)
    mixed[...] = jnp.concatenate(
        [m3[z, 8 * j:8 * j + 8, :] for z in range(NZ) for j in range(4)], axis=1).astype(BF16)
    drain(rl.at[pl.ds(0, NZ - 1)], recv.at[12])
    summed = jnp.sum(rl[...], axis=0)
    scale2 = lax.rsqrt(summed[:, 512:513] * (1.0 / 4096) + 1e-05)
    top = jnp.max(summed[:, 0:512], axis=1, keepdims=True) * scale2
    vr = iota((16, 128), 0)
    place = (4 * (t % 4) + (vr >> 2)) * 8 + 4 * c + (vr & 3)
    spread = jnp.where(iota((16, 128), 1) == place, top, LOW)
    mq[q] = jnp.max(spread, axis=0, keepdims=True)
    each(NQ, q, lambda k: push(mq.at[q], mq.at[q], at_q(k), send.at[13], recv.at[13]))
    drain(mq.at[pl.ds(0, NQ - 1)], recv.at[13])
    mz[mine_cz] = jnp.max(mq[:, 0, :], axis=0, keepdims=True)
    each(2 * NZ, mine_cz, lambda k: push(
        mz.at[mine_cz], mz.at[mine_cz], at_cz(k), send.at[14], recv.at[14]))
    drain(mz.at[pl.ds(0, 2 * NZ - 1)], recv.at[14])
    for k in range(2):
        both = [mz[m * NZ + 4 * k + n] for m in range(2) for n in range(4)]
        while len(both) > 1:
            both = [jnp.maximum(a, b) for a, b in zip(both[::2], both[1::2])]
        best[k:k + 1, :] = both[0]

    for n, (src, dst) in enumerate(pairs):
        drain(dst.at[c], bg_send.at[n])
    drain(hd.at[pl.ds(0, NZ - 1)], bg_send.at[4])
    drain(hd.at[pl.ds(0, NZ)], bg_send.at[5])
    sent = (
        at.at[pl.ds(0, NQ - 1)], pb.at[pl.ds(0, NZ - 1)], sb.at[pl.ds(0, NQ - 1)],
        eb.at[pl.ds(0, NZ - 1)], db.at[pl.ds(0, NY - 1)], g.at[0, pl.ds(0, NZ - 1)],
        g.at[pl.ds(0, NX - 1)], tb.at[pl.ds(0, NX - 1)], zb.at[pl.ds(0, NZ - 1)],
        yb.at[pl.ds(0, NY - 1)], mx.at[pl.ds(0, NZ - 1)], fr.at[pl.ds(0, NQ - 1)],
        lpb.at[pl.ds(0, NZ - 1)], mq.at[pl.ds(0, NQ - 1)], mz.at[pl.ds(0, 2 * NZ - 1)],
    )
    for n, ref in enumerate(sent):
        drain(ref, send.at[n])


def local(
    attn, resid, wo, norm_gain, router, expert_ids, w_gate, w_up, w_down, lengths, final_gain, head
):
    vm = pl.BlockSpec(memory_space=pltpu.VMEM)
    hbm = pl.BlockSpec(memory_space=pl.ANY)
    v = pltpu.VMEM
    dma = pltpu.SemaphoreType.DMA
    mixed, best = pl.pallas_call(
        kernel,
        out_shape=(
            jax.ShapeDtypeStruct((8, 4096), BF16),
            jax.ShapeDtypeStruct((2, 128), F32),
        ),
        in_specs=[hbm] * 12,
        out_specs=(vm, vm),
        scratch_shapes=[
            v((8, 4096), BF16), v((NQ, 128), F32), v((8, 4096), BF16), v((2, 8), jnp.int32),
            v((1, 4), jnp.int32), v((NQ, 128), F32),
            v((2, 64, 512), BF16), v((2, 4096, 128), BF16), v((2, 4096, 128), BF16),
            v((2, 128, 4096), BF16), v((16, 32, 512), BF16),
            v((NQ, 8, 512), BF16), v((NQ, 8, 128), F32), v((NZ, NQ, 128), F32),
            v((NZ, NQ, 128), F32), v((NQ, 1, 128), F32), v((NQ, 1, 128), F32),
            v((NQ, 128), F32), v((NZ, 8, 128), F32), v((NZ, 8, 128), F32),
            v((NY, 16, 128), BF16), v((NY, 16, 128), BF16), v((NX, NZ, 32, 512), BF16),
            v((4, 128, 128), F32), v((NX, NZ, 32, 512), BF16), v((NX, NZ, 32, 512), BF16),
            v((NZ, 32, 512), BF16), v((NZ, 32, 512), BF16), v((NY, 16, 128), BF16),
            v((NY, 16, 128), BF16), v((NZ, 32, 128), BF16), v((NQ, 16, 128), BF16),
            v((NZ, 16, 640), F32), v((NZ, 16, 640), F32), v((NQ, 1, 128), F32),
            v((2 * NZ, 1, 128), F32), v((4, 128, 512), BF16),
            dma((15,)), dma((15,)), dma((NZ,)), dma((NZ,)), dma((NZ,)),
            dma((6,)), dma((6,)), dma((6,)), dma((7,)),
        ],
        compiler_params=pltpu.CompilerParams(
            collective_id=0, has_side_effects=True, vmem_limit_bytes=63 << 20),
    )(
        attn, resid, wo.T, norm_gain.reshape(NQ, 128), router.T, expert_ids.T,
        w_gate, w_up, w_down, lengths, final_gain.reshape(NQ, 128), head,
    )
    return mixed, best.reshape(256)


def solution(mesh):
    placed = (
        P("ep", "tp"),
        P("ep", None),
        P("tp", "ep"),
        P(),
        P(),
        P("ep", None),
        P(None, ("ep", "tp")),
        P(None, ("ep", "tp")),
        P(("ep", "tp"), None),
        P("ep", None),
        P(),
        P(("ep", "tp"), None),
    )
    return jax.shard_map(
        local, mesh=mesh, in_specs=placed, out_specs=(P("ep", None), P()), check_vma=False
    )
```

```python
import jax
import jax.numpy as jnp
from jax import lax
from jax.experimental import pallas as pl
from jax.experimental.pallas import tpu as pltpu
from jax.sharding import PartitionSpec as P

F32 = jnp.float32
BF16 = jnp.bfloat16
NX, NY, NZ, NQ = 4, 8, 8, 32
MESH = pl.DeviceIdType.MESH
LOW = -3.0e38


def iota(shape, axis):
    return lax.broadcasted_iota(jnp.int32, shape, axis)


def mm(a, b):
    return jnp.dot(a, b, preferred_element_type=F32)


def near(i, t):
    half = (i + 1) // 2
    return (t + half * (2 * (i % 2) - 1) + NZ) % NZ


def kernel(
    attn, resid_in, wo, gain_in, router_in, ids_in, w_gate, w_up, w_down, lengths_in, fgain_in,
    head,
    mixed, best,
    resid, gain, router, ids, lengths, final_gain, wo2, wg2, wu2, wd2, hd,
    at, p3, pb, pr, sb, xb, x32, eb, rb,
    db, yd, g, acc, tb, xr, zb, zr, yb, yr, mx, fr, lpb, rl, mq, mz, order,
    send, recv, gz, gx, tx, bg_send, bg_recv, bg_local, small, g_left, g_right,
):
    ep = lax.axis_index("ep")
    t = lax.axis_index("tp")
    q = ep // 2
    c = ep % 2
    y = q // NX
    x = q % NX

    def at_q(k):
        return (2 * k + c, t)

    def at_z(k):
        return (ep, k)

    def at_y(k):
        return ((k * NX + x) * 2 + c, t)

    def at_x(k):
        return ((y * NX + k) * 2 + c, t)

    def at_cz(k):
        return (2 * q + k // NZ, k % NZ)

    other = (2 * q + 1 - c, t)
    mine_cz = c * NZ + t

    def each(count, me, body):
        def step(d, carry):
            body((me + d) % count)
            return carry

        lax.fori_loop(1, count, step, 0)

    def push(src, dst, where, send_sem, recv_sem):
        pltpu.make_async_remote_copy(
            src_ref=src, dst_ref=dst, send_sem=send_sem, recv_sem=recv_sem,
            device_id=where, device_id_type=MESH,
        ).start()

    def drain(ref, sem):
        pltpu.make_async_copy(ref, ref, sem).wait()

    inputs = (
        (attn, at.at[q]), (resid_in, resid), (gain_in, gain), (router_in, router),
        (ids_in, ids), (lengths_in, lengths), (fgain_in, final_gain),
    )
    for n, (src, dst) in enumerate(inputs):
        pltpu.make_async_copy(src, dst, small.at[n]).start()

    barrier = pltpu.get_barrier_semaphore()

    def hello(where):
        pl.semaphore_signal(barrier, inc=1, device_id=where, device_id_type=MESH)

    each(NQ, q, lambda k: hello(at_q(k)))
    each(2 * NZ, mine_cz, lambda k: hello(at_cz(k)))
    drain(at.at[q], small.at[0])
    pl.semaphore_wait(barrier, NQ - 1 + 2 * NZ - 1)

    each(NQ, q, lambda k: push(at.at[q], at.at[q], at_q(k), send.at[0], recv.at[0]))

    pairs = ((wo, wo2), (w_gate, wg2), (w_up, wu2), (w_down, wd2))

    def swap(n):
        src, dst = pairs[n]
        push(src, dst.at[c], other, bg_send.at[n], bg_recv.at[n])
        pltpu.make_async_copy(src, dst.at[c], bg_local.at[n]).start()

    swap(0)

    def head_part(k):
        return head.at[:, pl.ds(pl.multiple_of((k % NZ) * 512, 512), 512)]

    for n in range(1, len(inputs)):
        drain(inputs[n][1], small.at[n])

    rows = resid[...].astype(F32)
    row = jnp.sum(jnp.where(iota(rows.shape, 0) == t, rows, 0.0), axis=0, keepdims=True)
    for k in range(NQ):
        x32[k:k + 1, :] = row[:, 128 * k:128 * k + 128]

    eye = iota((8, 8), 0) == iota((8, 8), 1)
    id0 = jnp.sum(jnp.where(eye, ids[0:1, :], 0), axis=1, keepdims=True)
    id1 = jnp.sum(jnp.where(eye, ids[1:2, :], 0), axis=1, keepdims=True)
    id0_32 = jnp.concatenate([id0] * 4, axis=0)
    id1_32 = jnp.concatenate([id1] * 4, axis=0)
    r_i = iota((32, 128), 0)
    c_i = iota((32, 128), 1)
    col_k = c_i >> 4
    is0 = id0_32 == col_k
    is1 = id1_32 == col_k
    member = jnp.where(is0 | is1, 1.0, 0.0)
    lr = iota((32, 32), 0)
    lc = iota((32, 32), 1)
    lower = jnp.where(((lr >> 3) == (lc >> 3)) & (lc < lr), 1.0, 0.0)
    earlier = mm(lower.astype(BF16), member.astype(BF16))
    slot = (c_i & 3).astype(F32)
    placed = jnp.where(
        (jnp.abs(earlier - slot) < 0.5) & ((r_i >> 3) == ((c_i >> 2) & 3)), member, 0.0)
    ra = iota((128, 128), 0)
    ca = iota((128, 128), 1)
    perm = jnp.where(ca == 16 * ((ra >> 2) & 7) + 4 * (ra >> 5) + (ra & 3), 1.0, 0.0).astype(BF16)
    perm_t = jnp.where(ra == 16 * ((ca >> 2) & 7) + 4 * (ca >> 5) + (ca & 3), 1.0, 0.0).astype(BF16)

    lens = jnp.broadcast_to(lengths[...], (16, 4))
    ends = jnp.sum(
        jnp.where(iota((16, 4), 1) <= (iota((16, 4), 0) & 3), lens, 0), axis=1, keepdims=True) - 1
    sr = iota((16, 32), 0)
    sc = iota((16, 32), 1)
    pick = jnp.where(((sr >> 2) == (sc >> 3)) & (ends == (sc & 7)), 1.0, 0.0).astype(BF16)
    fa = iota((128, 512), 0)
    fb = iota((128, 512), 1) - 16 * (fa >> 2) - (fa & 3)
    for j in range(4):
        order[j] = jnp.where(fb == 4 * j, 1.0, 0.0).astype(BF16)

    drain(wo2.at[1 - c], bg_recv.at[0])
    drain(wo2.at[c], bg_local.at[0])
    drain(at.at[pl.ds(0, NQ - 1)], recv.at[0])
    for n in (1, 2, 3):
        swap(n)
    a = at[...].astype(F32).reshape(256, 512).astype(BF16)
    part = lax.dot_general(
        a, wo2[...].reshape(128, 512), (((1,), (1,)), ((), ())), preferred_element_type=F32)
    p3[...] = part.reshape(NQ, 8, 128)
    for r in range(NZ):
        pb[r] = p3[:, r, :]
    each(NZ, t, lambda k: push(pb.at[k], pr.at[t], at_z(k), send.at[1], recv.at[1]))
    pr[t] = pb[t]
    drain(pr.at[pl.ds(0, NZ - 1)], recv.at[1])
    sb[:, 0, :] = jnp.sum(pr[...], axis=0)
    each(NQ, q, lambda k: push(sb.at[k], xb.at[q], at_q(k), send.at[2], recv.at[2]))
    xb[q] = sb[q]
    drain(xb.at[pl.ds(0, NQ - 1)], recv.at[2])

    xrow = x32[...] + xb[:, 0, :]
    scale = lax.rsqrt(jnp.sum(xrow * xrow, keepdims=True) * (1.0 / 4096) + 1e-05)
    hrow = (xrow * scale * gain[...]).astype(BF16).astype(F32)
    lane = iota((1, 128), 1)
    x32[...] = hrow
    dots = jnp.zeros((8, 128), F32)
    for k in range(NQ):
        dots = dots + x32[k:k + 1, :] * router[:, 128 * k:128 * k + 128].astype(F32)
    x32[...] = xrow
    dots = jnp.sum(dots, axis=1, keepdims=True)
    put = jnp.where(iota((8, 128), 1) == iota((8, 128), 0) + 8, dots, 0.0)
    stats = jnp.where(lane == 0, scale, 0.0) + jnp.sum(put, axis=0, keepdims=True)
    eb[...] = jnp.zeros_like(eb)
    for k in range(NZ):
        eb[k, 0:4, :] = x32[4 * k:4 * k + 4, :]
        eb[k, 4:5, :] = stats
    each(NZ, t, lambda k: push(eb.at[k], rb.at[t], at_z(k), send.at[3], recv.at[3]))
    rb[t] = eb[t]
    drain(rb.at[pl.ds(0, NZ - 1)], recv.at[3])

    xs = jnp.concatenate([rb[:, j, :] for j in range(4)], axis=0)
    st = rb[:, 4, :]
    scale32 = jnp.concatenate([st[:, 0:1]] * 4, axis=0)
    gain32 = jnp.concatenate(
        [jnp.broadcast_to(gain[pl.ds(4 * t + j, 1), :], (8, 128)) for j in range(4)], axis=0)
    h32 = (xs * scale32 * gain32).astype(BF16)
    lane8 = iota((8, 128), 1)
    la = jnp.sum(jnp.where(lane8 == id0 + 8, st, 0.0), axis=1, keepdims=True)
    lb = jnp.sum(jnp.where(lane8 == id1 + 8, st, 0.0), axis=1, keepdims=True)
    wa = 1.0 / (1.0 + jnp.exp(lb - la))
    wb = 1.0 / (1.0 + jnp.exp(la - lb))
    wa32 = jnp.concatenate([wa] * 4, axis=0)
    wb32 = jnp.concatenate([wb] * 4, axis=0)
    combine = placed * jnp.where(is0, wa32, wb32)

    each(NZ, t, lambda k: push(
        head_part(k), hd.at[mine_cz], at_z(k), bg_send.at[4], bg_recv.at[4]))
    pltpu.make_async_copy(head_part(t), hd.at[mine_cz], bg_local.at[4]).start()

    disp = lax.dot_general(
        placed.astype(BF16), h32, (((0,), (0,)), ((), ())), preferred_element_type=F32)
    db[...] = disp.astype(BF16).reshape(NY, 16, 128)
    each(NY, y, lambda k: push(db.at[k], yd.at[y], at_y(k), send.at[4], recv.at[4]))
    yd[y] = db[y]
    drain(yd.at[pl.ds(0, NY - 1)], recv.at[4])
    slots = mm(perm, yd[...].reshape(128, 128)).astype(BF16)
    for j in range(4):
        g[x, t, :, 128 * j:128 * j + 128] = slots[32 * j:32 * j + 32, :]
    each(NZ, t, lambda k: push(g.at[x, t], g.at[x, t], at_z(k), send.at[5], gz.at[t]))
    right = (x + 1) % NX
    left = (x + NX - 1) % NX

    def spread_x(z):
        push(g.at[x, z], g.at[x, z], at_x(right), send.at[6], g_left.at[z])
        push(g.at[x, z], g.at[x, z], at_x(left), send.at[6], g_right.at[z])

    def pass_on(z):
        drain(g.at[left, z], g_left.at[z])
        part = g.at[left, z, pl.ds(0, 16)]
        push(part, part, at_x(right), send.at[15], gx.at[z])
        drain(g.at[right, z], g_right.at[z])
        part = g.at[right, z, pl.ds(16, 16)]
        push(part, part, at_x(left), send.at[15], gx.at[z])

    def arrive(i):
        z = near(i, t)
        drain(g.at[x, z], gz.at[z])
        spread_x(z)

    def forward(i, carry):
        arrive(i)
        pass_on(near(i - 2, t))
        return carry

    spread_x(t)
    arrive(1)
    lax.fori_loop(2, NZ, forward, 0)
    pass_on(near(NZ - 2, t))
    pass_on(near(NZ - 1, t))

    for n in (1, 2, 3):
        dst = pairs[n][1]
        drain(dst.at[1 - c], bg_recv.at[n])
        drain(dst.at[c], bg_local.at[n])
    acc[...] = jnp.zeros_like(acc)

    def up_step(i, carry):
        z = near(i, t)
        drain(g.at[0, z], gx.at[z])
        lhs = g[:, z].reshape(128, 512)
        start = pl.multiple_of(z * 512, 512)
        for k in range(2):
            acc[k] += mm(lhs, wg2[k, pl.ds(start, 512), :])
            acc[2 + k] += mm(lhs, wu2[k, pl.ds(start, 512), :])
        return carry

    lax.fori_loop(0, NZ, up_step, 0)
    hidden = jnp.concatenate(
        [acc[k] * jax.nn.sigmoid(acc[k]) * acc[2 + k] for k in range(2)], axis=1).astype(BF16)

    def down_step(i, carry):
        z = near(NZ - 1 - i, t)
        start = pl.multiple_of(z * 512, 512)
        term = mm(hidden, wd2[:, :, pl.ds(start, 512)].reshape(256, 512))
        tb[:, z] = term.reshape(NX, 32, 512).astype(BF16)
        each(NX, x, lambda k: push(tb.at[k, z], xr.at[x, z], at_x(k), send.at[7], tx.at[z]))
        xr[x, z] = tb[x, z]
        return carry

    lax.fori_loop(0, NZ, down_step, 0)

    def sum_x(z):
        drain(xr.at[pl.ds(0, NX - 1), z], tx.at[z])
        return jnp.sum(xr[:, z].astype(F32), axis=0).astype(BF16)

    def sum_step(i, carry):
        z = near(NZ - 1 - i, t)
        zb[z] = sum_x(z)
        push(zb.at[z], zr.at[t], at_z(z), send.at[8], recv.at[8])
        return carry

    lax.fori_loop(0, NZ - 1, sum_step, 0)
    zr[t] = sum_x(t)
    drain(zr.at[pl.ds(0, NZ - 1)], recv.at[8])
    total = jnp.sum(zr[...].astype(F32), axis=0)
    stacked = jnp.concatenate(
        [total[:, 128 * j:128 * j + 128] for j in range(4)], axis=0).astype(BF16)
    yb[...] = mm(perm_t, stacked).astype(BF16).reshape(NY, 16, 128)
    each(NY, y, lambda k: push(yb.at[k], yr.at[y], at_y(k), send.at[9], recv.at[9]))
    yr[y] = yb[y]
    drain(yr.at[pl.ds(0, NY - 1)], recv.at[9])

    mine = hd.at[pl.ds(c * NZ, NZ)]
    drain(hd.at[pl.ds(0, NZ - 1)], bg_recv.at[4])
    drain(hd.at[0], bg_local.at[4])
    push(mine, mine, other, bg_send.at[5], bg_recv.at[5])

    back = yr[...].reshape(128, 128).astype(F32)
    out32 = jnp.dot(combine, back, precision=lax.Precision.HIGHEST, preferred_element_type=F32)
    own = (xs + out32).astype(BF16)
    mx[t] = own
    fr[q] = mm(pick, own).astype(BF16)
    each(NQ, q, lambda k: push(fr.at[q], fr.at[q], at_q(k), send.at[11], recv.at[11]))
    each(NZ, t, lambda k: push(mx.at[t], mx.at[t], at_z(k), send.at[10], recv.at[10]))
    drain(mine, bg_recv.at[5])
    drain(fr.at[pl.ds(0, NQ - 1)], recv.at[11])

    rows512 = fr[...].reshape(512, 128)
    vocab = hd[...].reshape(512, 512)
    logits = jnp.zeros((128, 512), F32)
    squares = jnp.zeros((128, 128), F32)
    for j in range(4):
        rows_j = mm(order[j], rows512)
        squares = squares + rows_j * rows_j
        fin = (rows_j * final_gain[pl.ds(4 * t + j, 1), :]).astype(BF16)
        logits = logits + lax.dot_general(
            fin, vocab[:, 128 * j:128 * j + 128], (((1,), (1,)), ((), ())),
            preferred_element_type=F32)
    squares = jnp.broadcast_to(jnp.sum(squares, axis=1, keepdims=True), (128, 128))
    lpb[:, :, 0:512] = logits.reshape(NZ, 16, 512).astype(BF16)
    lpb[:, :, 512:640] = squares.reshape(NZ, 16, 128).astype(BF16)
    each(NZ, t, lambda k: push(lpb.at[k], rl.at[t], at_z(k), send.at[12], recv.at[12]))
    rl[t] = lpb[t]
    drain(mx.at[pl.ds(0, NZ - 1)], recv.at[10])
    m3 = mx[...].astype(F32)
    mixed[...] = jnp.concatenate(
        [m3[z, 8 * j:8 * j + 8, :] for z in range(NZ) for j in range(4)], axis=1).astype(BF16)
    drain(rl.at[pl.ds(0, NZ - 1)], recv.at[12])
    summed = jnp.sum(rl[...].astype(F32), axis=0)
    scale2 = lax.rsqrt(summed[:, 512:513] * (1.0 / 4096) + 1e-05)
    top = jnp.max(summed[:, 0:512], axis=1, keepdims=True) * scale2
    vr = iota((16, 128), 0)
    place = (4 * (t % 4) + (vr >> 2)) * 8 + 4 * c + (vr & 3)
    spread = jnp.where(iota((16, 128), 1) == place, top, LOW)
    mq[q] = jnp.max(spread, axis=0, keepdims=True)
    each(NQ, q, lambda k: push(mq.at[q], mq.at[q], at_q(k), send.at[13], recv.at[13]))
    drain(mq.at[pl.ds(0, NQ - 1)], recv.at[13])
    mz[mine_cz] = jnp.max(mq[:, 0, :], axis=0, keepdims=True)
    each(2 * NZ, mine_cz, lambda k: push(
        mz.at[mine_cz], mz.at[mine_cz], at_cz(k), send.at[14], recv.at[14]))
    drain(mz.at[pl.ds(0, 2 * NZ - 1)], recv.at[14])
    for k in range(2):
        both = [mz[m * NZ + 4 * k + n] for m in range(2) for n in range(4)]
        while len(both) > 1:
            both = [jnp.maximum(a, b) for a, b in zip(both[::2], both[1::2])]
        best[k:k + 1, :] = both[0]

    for n, (src, dst) in enumerate(pairs):
        drain(dst.at[c], bg_send.at[n])
    drain(hd.at[pl.ds(0, NZ - 1)], bg_send.at[4])
    drain(hd.at[pl.ds(0, NZ)], bg_send.at[5])
    sent = (
        at.at[pl.ds(0, NQ - 1)], pb.at[pl.ds(0, NZ - 1)], sb.at[pl.ds(0, NQ - 1)],
        eb.at[pl.ds(0, NZ - 1)], db.at[pl.ds(0, NY - 1)], g.at[0, pl.ds(0, NZ - 1)],
        g.at[pl.ds(0, 2)], tb.at[pl.ds(0, NX - 1)], zb.at[pl.ds(0, NZ - 1)],
        yb.at[pl.ds(0, NY - 1)], mx.at[pl.ds(0, NZ - 1)], fr.at[pl.ds(0, NQ - 1)],
        lpb.at[pl.ds(0, NZ - 1)], mq.at[pl.ds(0, NQ - 1)], mz.at[pl.ds(0, 2 * NZ - 1)],
        g.at[0],
    )
    for n, ref in enumerate(sent):
        drain(ref, send.at[n])


def local(
    attn, resid, wo, norm_gain, router, expert_ids, w_gate, w_up, w_down, lengths, final_gain, head
):
    vm = pl.BlockSpec(memory_space=pltpu.VMEM)
    hbm = pl.BlockSpec(memory_space=pl.ANY)
    v = pltpu.VMEM
    dma = pltpu.SemaphoreType.DMA
    mixed, best = pl.pallas_call(
        kernel,
        out_shape=(
            jax.ShapeDtypeStruct((8, 4096), BF16),
            jax.ShapeDtypeStruct((2, 128), F32),
        ),
        in_specs=[hbm] * 12,
        out_specs=(vm, vm),
        scratch_shapes=[
            v((8, 4096), BF16), v((NQ, 128), F32), v((8, 4096), BF16), v((2, 8), jnp.int32),
            v((1, 4), jnp.int32), v((NQ, 128), F32),
            v((2, 64, 512), BF16), v((2, 4096, 128), BF16), v((2, 4096, 128), BF16),
            v((2, 128, 4096), BF16), v((16, 32, 512), BF16),
            v((NQ, 8, 512), BF16), v((NQ, 8, 128), F32), v((NZ, NQ, 128), F32),
            v((NZ, NQ, 128), F32), v((NQ, 1, 128), F32), v((NQ, 1, 128), F32),
            v((NQ, 128), F32), v((NZ, 8, 128), F32), v((NZ, 8, 128), F32),
            v((NY, 16, 128), BF16), v((NY, 16, 128), BF16), v((NX, NZ, 32, 512), BF16),
            v((4, 128, 128), F32), v((NX, NZ, 32, 512), BF16), v((NX, NZ, 32, 512), BF16),
            v((NZ, 32, 512), BF16), v((NZ, 32, 512), BF16), v((NY, 16, 128), BF16),
            v((NY, 16, 128), BF16), v((NZ, 32, 128), BF16), v((NQ, 16, 128), BF16),
            v((NZ, 16, 640), BF16), v((NZ, 16, 640), BF16), v((NQ, 1, 128), F32),
            v((2 * NZ, 1, 128), F32), v((4, 128, 512), BF16),
            dma((16,)), dma((15,)), dma((NZ,)), dma((NZ,)), dma((NZ,)),
            dma((6,)), dma((6,)), dma((6,)), dma((7,)), dma((NZ,)), dma((NZ,)),
        ],
        compiler_params=pltpu.CompilerParams(
            collective_id=0, has_side_effects=True, vmem_limit_bytes=63 << 20),
    )(
        attn, resid, wo.T, norm_gain.reshape(NQ, 128), router.T, expert_ids.T,
        w_gate, w_up, w_down, lengths, final_gain.reshape(NQ, 128), head,
    )
    return mixed, best.reshape(256)


def solution(mesh):
    placed = (
        P("ep", "tp"),
        P("ep", None),
        P("tp", "ep"),
        P(),
        P(),
        P("ep", None),
        P(None, ("ep", "tp")),
        P(None, ("ep", "tp")),
        P(("ep", "tp"), None),
        P("ep", None),
        P(),
        P(("ep", "tp"), None),
    )
    return jax.shard_map(
        local, mesh=mesh, in_specs=placed, out_specs=(P("ep", None), P()), check_vma=False
    )
```

```python
import jax
import jax.numpy as jnp
from jax import lax
from jax.experimental import pallas as pl
from jax.experimental.pallas import tpu as pltpu
from jax.sharding import PartitionSpec as P

F32 = jnp.float32
BF16 = jnp.bfloat16
NX, NY, NZ, NQ = 4, 8, 8, 32
MESH = pl.DeviceIdType.MESH
LOW = -3.0e38


def iota(shape, axis):
    return lax.broadcasted_iota(jnp.int32, shape, axis)


def mm(a, b):
    return jnp.dot(a, b, preferred_element_type=F32)


def near(i, t):
    half = (i + 1) // 2
    return (t + half * (2 * (i % 2) - 1) + NZ) % NZ


def kernel(
    attn, resid_in, wo, gain_in, router_in, ids_in, w_gate, w_up, w_down, lengths_in, fgain_in,
    head,
    mixed, best,
    resid, gain, router, ids, lengths, final_gain, wo2, wg2, wu2, wd2, hd,
    at, p3, pb, pr, sb, xb, x32, eb, rb,
    db, yd, g, acc, tb, xr, zb, zr, yb, yr, mx, fr, lpb, rl, mq, mz, order,
    send, recv, gz, gx, tx, bg_send, bg_recv, bg_local, small,
):
    ep = lax.axis_index("ep")
    t = lax.axis_index("tp")
    q = ep // 2
    c = ep % 2
    y = q // NX
    x = q % NX

    def at_q(k):
        return (2 * k + c, t)

    def at_z(k):
        return (ep, k)

    def at_y(k):
        return ((k * NX + x) * 2 + c, t)

    def at_x(k):
        return ((y * NX + k) * 2 + c, t)

    def at_cz(k):
        return (2 * q + k // NZ, k % NZ)

    other = (2 * q + 1 - c, t)
    mine_cz = c * NZ + t

    def each(count, me, body):
        def step(d, carry):
            body((me + d) % count)
            return carry

        lax.fori_loop(1, count, step, 0)

    def push(src, dst, where, send_sem, recv_sem):
        pltpu.make_async_remote_copy(
            src_ref=src, dst_ref=dst, send_sem=send_sem, recv_sem=recv_sem,
            device_id=where, device_id_type=MESH,
        ).start()

    def drain(ref, sem):
        pltpu.make_async_copy(ref, ref, sem).wait()

    inputs = (
        (attn, at.at[q]), (resid_in, resid), (gain_in, gain), (router_in, router),
        (ids_in, ids), (lengths_in, lengths), (fgain_in, final_gain),
    )
    for n, (src, dst) in enumerate(inputs):
        pltpu.make_async_copy(src, dst, small.at[n]).start()

    barrier = pltpu.get_barrier_semaphore()

    def hello(where):
        pl.semaphore_signal(barrier, inc=1, device_id=where, device_id_type=MESH)

    each(NQ, q, lambda k: hello(at_q(k)))
    each(2 * NZ, mine_cz, lambda k: hello(at_cz(k)))
    drain(at.at[q], small.at[0])
    pl.semaphore_wait(barrier, NQ - 1 + 2 * NZ - 1)

    each(NQ, q, lambda k: push(at.at[q], at.at[q], at_q(k), send.at[0], recv.at[0]))

    pairs = ((wo, wo2), (w_gate, wg2), (w_up, wu2), (w_down, wd2))

    def swap(n):
        src, dst = pairs[n]
        push(src, dst.at[c], other, bg_send.at[n], bg_recv.at[n])
        pltpu.make_async_copy(src, dst.at[c], bg_local.at[n]).start()

    swap(0)

    def head_part(k):
        return head.at[:, pl.ds(pl.multiple_of((k % NZ) * 512, 512), 512)]

    each(NZ, t, lambda k: push(
        head_part(k), hd.at[mine_cz], at_z(k), bg_send.at[4], bg_recv.at[4]))
    pltpu.make_async_copy(head_part(t), hd.at[mine_cz], bg_local.at[4]).start()

    for n in range(1, len(inputs)):
        drain(inputs[n][1], small.at[n])

    rows = resid[...].astype(F32)
    row = jnp.sum(jnp.where(iota(rows.shape, 0) == t, rows, 0.0), axis=0, keepdims=True)
    for k in range(NQ):
        x32[k:k + 1, :] = row[:, 128 * k:128 * k + 128]

    eye = iota((8, 8), 0) == iota((8, 8), 1)
    id0 = jnp.sum(jnp.where(eye, ids[0:1, :], 0), axis=1, keepdims=True)
    id1 = jnp.sum(jnp.where(eye, ids[1:2, :], 0), axis=1, keepdims=True)
    id0_32 = jnp.concatenate([id0] * 4, axis=0)
    id1_32 = jnp.concatenate([id1] * 4, axis=0)
    r_i = iota((32, 128), 0)
    c_i = iota((32, 128), 1)
    col_k = c_i >> 4
    is0 = id0_32 == col_k
    is1 = id1_32 == col_k
    member = jnp.where(is0 | is1, 1.0, 0.0)
    lr = iota((32, 32), 0)
    lc = iota((32, 32), 1)
    lower = jnp.where(((lr >> 3) == (lc >> 3)) & (lc < lr), 1.0, 0.0)
    earlier = mm(lower.astype(BF16), member.astype(BF16))
    slot = (c_i & 3).astype(F32)
    placed = jnp.where(
        (jnp.abs(earlier - slot) < 0.5) & ((r_i >> 3) == ((c_i >> 2) & 3)), member, 0.0)
    ra = iota((128, 128), 0)
    ca = iota((128, 128), 1)
    perm = jnp.where(ca == 16 * ((ra >> 2) & 7) + 4 * (ra >> 5) + (ra & 3), 1.0, 0.0).astype(BF16)
    perm_t = jnp.where(ra == 16 * ((ca >> 2) & 7) + 4 * (ca >> 5) + (ca & 3), 1.0, 0.0).astype(BF16)

    lens = jnp.broadcast_to(lengths[...], (16, 4))
    ends = jnp.sum(
        jnp.where(iota((16, 4), 1) <= (iota((16, 4), 0) & 3), lens, 0), axis=1, keepdims=True) - 1
    sr = iota((16, 32), 0)
    sc = iota((16, 32), 1)
    pick = jnp.where(((sr >> 2) == (sc >> 3)) & (ends == (sc & 7)), 1.0, 0.0).astype(BF16)
    fa = iota((128, 512), 0)
    fb = iota((128, 512), 1) - 16 * (fa >> 2) - (fa & 3)
    for j in range(4):
        order[j] = jnp.where(fb == 4 * j, 1.0, 0.0).astype(BF16)

    drain(wo2.at[1 - c], bg_recv.at[0])
    drain(wo2.at[c], bg_local.at[0])
    drain(at.at[pl.ds(0, NQ - 1)], recv.at[0])
    for n in (1, 2, 3):
        swap(n)
    a = at[...].astype(F32).reshape(256, 512).astype(BF16)
    part = lax.dot_general(
        a, wo2[...].reshape(128, 512), (((1,), (1,)), ((), ())), preferred_element_type=F32)
    p3[...] = part.reshape(NQ, 8, 128)
    for r in range(NZ):
        pb[r] = p3[:, r, :]
    each(NZ, t, lambda k: push(pb.at[k], pr.at[t], at_z(k), send.at[1], recv.at[1]))
    pr[t] = pb[t]
    drain(pr.at[pl.ds(0, NZ - 1)], recv.at[1])
    sb[:, 0, :] = jnp.sum(pr[...], axis=0)
    each(NQ, q, lambda k: push(sb.at[k], xb.at[q], at_q(k), send.at[2], recv.at[2]))
    xb[q] = sb[q]
    drain(xb.at[pl.ds(0, NQ - 1)], recv.at[2])

    xrow = x32[...] + xb[:, 0, :]
    scale = lax.rsqrt(jnp.sum(xrow * xrow, keepdims=True) * (1.0 / 4096) + 1e-05)
    hrow = (xrow * scale * gain[...]).astype(BF16).astype(F32)
    lane = iota((1, 128), 1)
    x32[...] = hrow
    dots = jnp.zeros((8, 128), F32)
    for k in range(NQ):
        dots = dots + x32[k:k + 1, :] * router[:, 128 * k:128 * k + 128].astype(F32)
    x32[...] = xrow
    dots = jnp.sum(dots, axis=1, keepdims=True)
    put = jnp.where(iota((8, 128), 1) == iota((8, 128), 0) + 8, dots, 0.0)
    stats = jnp.where(lane == 0, scale, 0.0) + jnp.sum(put, axis=0, keepdims=True)
    eb[...] = jnp.zeros_like(eb)
    for k in range(NZ):
        eb[k, 0:4, :] = x32[4 * k:4 * k + 4, :]
        eb[k, 4:5, :] = stats
    each(NZ, t, lambda k: push(eb.at[k], rb.at[t], at_z(k), send.at[3], recv.at[3]))
    rb[t] = eb[t]
    drain(rb.at[pl.ds(0, NZ - 1)], recv.at[3])

    xs = jnp.concatenate([rb[:, j, :] for j in range(4)], axis=0)
    st = rb[:, 4, :]
    scale32 = jnp.concatenate([st[:, 0:1]] * 4, axis=0)
    gain32 = jnp.concatenate(
        [jnp.broadcast_to(gain[pl.ds(4 * t + j, 1), :], (8, 128)) for j in range(4)], axis=0)
    h32 = (xs * scale32 * gain32).astype(BF16)
    lane8 = iota((8, 128), 1)
    la = jnp.sum(jnp.where(lane8 == id0 + 8, st, 0.0), axis=1, keepdims=True)
    lb = jnp.sum(jnp.where(lane8 == id1 + 8, st, 0.0), axis=1, keepdims=True)
    wa = 1.0 / (1.0 + jnp.exp(lb - la))
    wb = 1.0 / (1.0 + jnp.exp(la - lb))
    wa32 = jnp.concatenate([wa] * 4, axis=0)
    wb32 = jnp.concatenate([wb] * 4, axis=0)
    combine = placed * jnp.where(is0, wa32, wb32)

    disp = lax.dot_general(
        placed.astype(BF16), h32, (((0,), (0,)), ((), ())), preferred_element_type=F32)
    db[...] = disp.astype(BF16).reshape(NY, 16, 128)
    each(NY, y, lambda k: push(db.at[k], yd.at[y], at_y(k), send.at[4], recv.at[4]))
    yd[y] = db[y]
    drain(yd.at[pl.ds(0, NY - 1)], recv.at[4])
    slots = mm(perm, yd[...].reshape(128, 128)).astype(BF16)
    for j in range(4):
        g[x, t, :, 128 * j:128 * j + 128] = slots[32 * j:32 * j + 32, :]
    each(NZ, t, lambda k: push(g.at[x, t], g.at[x, t], at_z(k), send.at[5], gz.at[t]))
    each(NX, x, lambda k: push(g.at[x, t], g.at[x, t], at_x(k), send.at[6], gx.at[t]))

    def forward(i, carry):
        z = near(i, t)
        drain(g.at[x, z], gz.at[z])
        each(NX, x, lambda k: push(g.at[x, z], g.at[x, z], at_x(k), send.at[6], gx.at[z]))
        return carry

    lax.fori_loop(1, NZ, forward, 0)

    for n in (1, 2, 3):
        dst = pairs[n][1]
        drain(dst.at[1 - c], bg_recv.at[n])
        drain(dst.at[c], bg_local.at[n])
    acc[...] = jnp.zeros_like(acc)

    def up_step(i, carry):
        z = near(i, t)
        drain(g.at[pl.ds(0, NX - 1), z], gx.at[z])
        lhs = g[:, z].reshape(128, 512)
        start = pl.multiple_of(z * 512, 512)
        for k in range(2):
            acc[k] += mm(lhs, wg2[k, pl.ds(start, 512), :])
            acc[2 + k] += mm(lhs, wu2[k, pl.ds(start, 512), :])
        return carry

    lax.fori_loop(0, NZ, up_step, 0)
    hidden = jnp.concatenate(
        [acc[k] * jax.nn.sigmoid(acc[k]) * acc[2 + k] for k in range(2)], axis=1).astype(BF16)

    def down_step(i, carry):
        z = near(NZ - 1 - i, t)
        start = pl.multiple_of(z * 512, 512)
        term = mm(hidden, wd2[:, :, pl.ds(start, 512)].reshape(256, 512))
        tb[:, z] = term.reshape(NX, 32, 512).astype(BF16)
        each(NX, x, lambda k: push(tb.at[k, z], xr.at[x, z], at_x(k), send.at[7], tx.at[z]))
        xr[x, z] = tb[x, z]
        return carry

    lax.fori_loop(0, NZ, down_step, 0)

    def sum_x(z):
        drain(xr.at[pl.ds(0, NX - 1), z], tx.at[z])
        return jnp.sum(xr[:, z].astype(F32), axis=0).astype(BF16)

    def sum_step(i, carry):
        z = near(NZ - 1 - i, t)
        zb[z] = sum_x(z)
        push(zb.at[z], zr.at[t], at_z(z), send.at[8], recv.at[8])
        return carry

    lax.fori_loop(0, NZ - 1, sum_step, 0)
    zr[t] = sum_x(t)
    drain(zr.at[pl.ds(0, NZ - 1)], recv.at[8])
    total = jnp.sum(zr[...].astype(F32), axis=0)
    stacked = jnp.concatenate(
        [total[:, 128 * j:128 * j + 128] for j in range(4)], axis=0).astype(BF16)
    yb[...] = mm(perm_t, stacked).astype(BF16).reshape(NY, 16, 128)
    each(NY, y, lambda k: push(yb.at[k], yr.at[y], at_y(k), send.at[9], recv.at[9]))
    yr[y] = yb[y]
    drain(yr.at[pl.ds(0, NY - 1)], recv.at[9])

    mine = hd.at[pl.ds(c * NZ, NZ)]
    drain(hd.at[pl.ds(0, NZ - 1)], bg_recv.at[4])
    drain(hd.at[0], bg_local.at[4])
    push(mine, mine, other, bg_send.at[5], bg_recv.at[5])

    back = yr[...].reshape(128, 128).astype(F32)
    out32 = jnp.dot(combine, back, precision=lax.Precision.HIGHEST, preferred_element_type=F32)
    own = (xs + out32).astype(BF16)
    mx[t] = own
    fr[q] = mm(pick, own).astype(BF16)
    each(NQ, q, lambda k: push(fr.at[q], fr.at[q], at_q(k), send.at[11], recv.at[11]))
    each(NZ, t, lambda k: push(mx.at[t], mx.at[t], at_z(k), send.at[10], recv.at[10]))
    drain(mine, bg_recv.at[5])
    drain(fr.at[pl.ds(0, NQ - 1)], recv.at[11])

    rows512 = fr[...].reshape(512, 128)
    vocab = hd[...].reshape(512, 512)
    logits = jnp.zeros((128, 512), F32)
    squares = jnp.zeros((128, 128), F32)
    for j in range(4):
        rows_j = mm(order[j], rows512)
        squares = squares + rows_j * rows_j
        fin = (rows_j * final_gain[pl.ds(4 * t + j, 1), :]).astype(BF16)
        logits = logits + lax.dot_general(
            fin, vocab[:, 128 * j:128 * j + 128], (((1,), (1,)), ((), ())),
            preferred_element_type=F32)
    squares = jnp.broadcast_to(jnp.sum(squares, axis=1, keepdims=True), (128, 128))
    lpb[:, :, 0:512] = logits.reshape(NZ, 16, 512).astype(BF16)
    lpb[:, :, 512:640] = squares.reshape(NZ, 16, 128).astype(BF16)
    each(NZ, t, lambda k: push(lpb.at[k], rl.at[t], at_z(k), send.at[12], recv.at[12]))
    rl[t] = lpb[t]
    drain(mx.at[pl.ds(0, NZ - 1)], recv.at[10])
    m3 = mx[...].astype(F32)
    mixed[...] = jnp.concatenate(
        [m3[z, 8 * j:8 * j + 8, :] for z in range(NZ) for j in range(4)], axis=1).astype(BF16)
    drain(rl.at[pl.ds(0, NZ - 1)], recv.at[12])
    summed = jnp.sum(rl[...].astype(F32), axis=0)
    scale2 = lax.rsqrt(summed[:, 512:513] * (1.0 / 4096) + 1e-05)
    top = jnp.max(summed[:, 0:512], axis=1, keepdims=True) * scale2
    vr = iota((16, 128), 0)
    place = (4 * (t % 4) + (vr >> 2)) * 8 + 4 * c + (vr & 3)
    spread = jnp.where(iota((16, 128), 1) == place, top, LOW)
    mq[q] = jnp.max(spread, axis=0, keepdims=True)
    each(NQ, q, lambda k: push(mq.at[q], mq.at[q], at_q(k), send.at[13], recv.at[13]))
    drain(mq.at[pl.ds(0, NQ - 1)], recv.at[13])
    mz[mine_cz] = jnp.max(mq[:, 0, :], axis=0, keepdims=True)
    each(2 * NZ, mine_cz, lambda k: push(
        mz.at[mine_cz], mz.at[mine_cz], at_cz(k), send.at[14], recv.at[14]))
    drain(mz.at[pl.ds(0, 2 * NZ - 1)], recv.at[14])
    for k in range(2):
        both = [mz[m * NZ + 4 * k + n] for m in range(2) for n in range(4)]
        while len(both) > 1:
            both = [jnp.maximum(a, b) for a, b in zip(both[::2], both[1::2])]
        best[k:k + 1, :] = both[0]

    for n, (src, dst) in enumerate(pairs):
        drain(dst.at[c], bg_send.at[n])
    drain(hd.at[pl.ds(0, NZ - 1)], bg_send.at[4])
    drain(hd.at[pl.ds(0, NZ)], bg_send.at[5])
    sent = (
        at.at[pl.ds(0, NQ - 1)], pb.at[pl.ds(0, NZ - 1)], sb.at[pl.ds(0, NQ - 1)],
        eb.at[pl.ds(0, NZ - 1)], db.at[pl.ds(0, NY - 1)], g.at[0, pl.ds(0, NZ - 1)],
        g.at[pl.ds(0, NX - 1)], tb.at[pl.ds(0, NX - 1)], zb.at[pl.ds(0, NZ - 1)],
        yb.at[pl.ds(0, NY - 1)], mx.at[pl.ds(0, NZ - 1)], fr.at[pl.ds(0, NQ - 1)],
        lpb.at[pl.ds(0, NZ - 1)], mq.at[pl.ds(0, NQ - 1)], mz.at[pl.ds(0, 2 * NZ - 1)],
    )
    for n, ref in enumerate(sent):
        drain(ref, send.at[n])


def local(
    attn, resid, wo, norm_gain, router, expert_ids, w_gate, w_up, w_down, lengths, final_gain, head
):
    vm = pl.BlockSpec(memory_space=pltpu.VMEM)
    hbm = pl.BlockSpec(memory_space=pl.ANY)
    v = pltpu.VMEM
    dma = pltpu.SemaphoreType.DMA
    mixed, best = pl.pallas_call(
        kernel,
        out_shape=(
            jax.ShapeDtypeStruct((8, 4096), BF16),
            jax.ShapeDtypeStruct((2, 128), F32),
        ),
        in_specs=[hbm] * 12,
        out_specs=(vm, vm),
        scratch_shapes=[
            v((8, 4096), BF16), v((NQ, 128), F32), v((8, 4096), BF16), v((2, 8), jnp.int32),
            v((1, 4), jnp.int32), v((NQ, 128), F32),
            v((2, 64, 512), BF16), v((2, 4096, 128), BF16), v((2, 4096, 128), BF16),
            v((2, 128, 4096), BF16), v((16, 32, 512), BF16),
            v((NQ, 8, 512), BF16), v((NQ, 8, 128), F32), v((NZ, NQ, 128), F32),
            v((NZ, NQ, 128), F32), v((NQ, 1, 128), F32), v((NQ, 1, 128), F32),
            v((NQ, 128), F32), v((NZ, 8, 128), F32), v((NZ, 8, 128), F32),
            v((NY, 16, 128), BF16), v((NY, 16, 128), BF16), v((NX, NZ, 32, 512), BF16),
            v((4, 128, 128), F32), v((NX, NZ, 32, 512), BF16), v((NX, NZ, 32, 512), BF16),
            v((NZ, 32, 512), BF16), v((NZ, 32, 512), BF16), v((NY, 16, 128), BF16),
            v((NY, 16, 128), BF16), v((NZ, 32, 128), BF16), v((NQ, 16, 128), BF16),
            v((NZ, 16, 640), BF16), v((NZ, 16, 640), BF16), v((NQ, 1, 128), F32),
            v((2 * NZ, 1, 128), F32), v((4, 128, 512), BF16),
            dma((15,)), dma((15,)), dma((NZ,)), dma((NZ,)), dma((NZ,)),
            dma((6,)), dma((6,)), dma((6,)), dma((7,)),
        ],
        compiler_params=pltpu.CompilerParams(
            collective_id=0, has_side_effects=True, vmem_limit_bytes=63 << 20),
    )(
        attn, resid, wo.T, norm_gain.reshape(NQ, 128), router.T, expert_ids.T,
        w_gate, w_up, w_down, lengths, final_gain.reshape(NQ, 128), head,
    )
    return mixed, best.reshape(256)


def solution(mesh):
    placed = (
        P("ep", "tp"),
        P("ep", None),
        P("tp", "ep"),
        P(),
        P(),
        P("ep", None),
        P(None, ("ep", "tp")),
        P(None, ("ep", "tp")),
        P(("ep", "tp"), None),
        P("ep", None),
        P(),
        P(("ep", "tp"), None),
    )
    return jax.shard_map(
        local, mesh=mesh, in_specs=placed, out_specs=(P("ep", None), P()), check_vma=False
    )
```
